32 devices in a mesh: dp: 16 (over z, y, x), tensor: 2 (over core).
Axes of the slice: x: 2, y: 2, z: 4, core: 2. Of those that a mesh axis runs over, the one named last changes fastest.
Arguments:
- hidden_in: bfloat16 [4096, 1024], P(('dp', 'tensor')), may hold values from -6 to 6
- positions: int32 [4096], P('dp'), may hold values from 0 to 255, as said below
- w_query: bfloat16 [1024, 2048], P('dp', 'tensor'), may hold values from -0.1875 to 0.1875
- key_projection_weight: bfloat16 [1024, 1024], P('dp', 'tensor'), may hold values from -0.1875 to 0.1875
- value_projection_weight: bfloat16 [1024, 1024], P('dp', 'tensor'), may hold values from -0.1875 to 0.1875
- w_output: bfloat16 [2048, 1024], P('tensor', 'dp'), may hold values from -0.375 to 0.375
- w_gate: bfloat16 [1024, 3072], P('dp', 'tensor'), may hold values from -0.1875 to 0.1875
- w_up: bfloat16 [1024, 3072], P('dp', 'tensor'), may hold values from -0.1875 to 0.1875
- w_down: bfloat16 [3072, 1024], P('tensor', 'dp'), may hold values from -0.109375 to 0.109375
- norm_gains: float32 [2304], P('dp'), may hold values from 0.4 to 3
- grad_out: bfloat16 [4096, 1024], P(('dp', 'tensor')), may hold values from -8 to 8
Outputs:
- hidden_out: bfloat16 [4096, 1024], P(('dp', 'tensor'))
- grad_in: bfloat16 [4096, 1024], P(('dp', 'tensor'))
- grad_query: float32 [1024, 2048], P('dp', 'tensor')
- grad_key: float32 [1024, 1024], P('dp', 'tensor')
- grad_value: float32 [1024, 1024], P('dp', 'tensor')
- grad_output: float32 [2048, 1024], P('tensor', 'dp')
- grad_gate: float32 [1024, 3072], P('dp', 'tensor')
- grad_up: float32 [1024, 3072], P('dp', 'tensor')
- grad_down: float32 [3072, 1024], P('tensor', 'dp')
- grad_gains: float32 [2304], P(('dp', 'tensor'))
The draws below stay inside these ranges and needn't reach their ends.
Inputs may be any that keep to these rules, and one draw needn't show every extreme that they name: `positions`: positions count 0, 1, 2, ... along each sequence; a sequence starts where a position is 0; each index of dp holds whole sequences in its 256 tokens, and in some index one sequence fills all of them.
All inputs are finite; a program needn't handle non-finite values.
Results may differ from the reference program's by a relative error of at most 0.035.
Values may be sent and summed in bfloat16 or wider, within the bound.
No kernel may reach another device: no remote copies, remote signals or barrier semaphores. Data moves between devices by JAX's collectives and lax.ppermute only.
A program may use at most 128 MiB of HBM per device.

```python
import math
import jax
import jax.numpy as jnp
from jax import lax

MODEL_WIDTH = 1024
QUERY_HEADS = 16
KEY_VALUE_HEADS = 8
HEAD_SIZE = 128
FF = 3072
GROUP = 256
TOKENS = 4096
GAINS = 2304


def draw_positions(key, part):
    first, second, third = jax.random.split(jax.random.fold_in(key, 7), 3)
    group_count = TOKENS // GROUP
    rate_shift = jax.random.randint(first, (group_count, 1), 2, 9)
    coins = jax.random.randint(second, (group_count, GROUP), 0, 65536)
    threshold = jnp.right_shift(jnp.int32(65536), rate_shift)
    index = jnp.arange(GROUP, dtype=jnp.int32)[None, :]
    starts = (coins < threshold) | (index == 0)
    filled = jax.random.randint(third, (), 0, group_count)
    group_index = jnp.arange(group_count, dtype=jnp.int32)[:, None]
    starts = jnp.where(group_index == filled, index == 0, starts)
    last_start = lax.cummax(jnp.where(starts, index, 0), axis=1)
    return (index - last_start).reshape(TOKENS).astype(jnp.int32)


def draw_norm_gains(key, part):
    first = jax.random.fold_in(jax.random.fold_in(key, 5), 0)
    return jnp.exp(jax.random.uniform(first, (GAINS,), jnp.float32, -0.6, 0.6))


def draw_grad_out(key, part):
    first = jax.random.fold_in(jax.random.fold_in(key, 9), 0)
    third = jax.random.fold_in(jax.random.fold_in(key, 9), 2)
    ramp = jnp.arange(TOKENS, dtype=jnp.float32)[:, None] / TOKENS
    jitter = jax.random.uniform(third, (TOKENS, 1), jnp.float32, 0.7, 1.4)
    values = jax.random.normal(first, (TOKENS, MODEL_WIDTH), jnp.float32) * 0.6 * jnp.power(3.0, ramp) * jitter
    return jnp.clip(values, -8.0, 8.0).astype(jnp.bfloat16)


def block_levels(stream_key, shape, pieces, least, high):
    def one(axis_at, parts):
        heights = jax.random.uniform(jax.random.fold_in(jax.random.fold_in(stream_key, 6), axis_at), (parts,), jnp.float32, least / len(pieces), high / len(pieces))
        return jnp.repeat(jnp.exp(heights), shape[axis_at] // parts).reshape((-1,) + (1,) * (len(shape) - axis_at - 1))

    level = one(*pieces[0])
    for cut in pieces[1:]:
        level = level * one(*cut)
    return level


def scatter_about(stream_key, dims, width, reach, cuts=(), held_as=jnp.bfloat16):
    array = width * jax.random.normal(stream_key, dims, jnp.float32)
    if cuts:
        array = array * block_levels(stream_key, dims, cuts, -0.22, 0.18)
    return jnp.clip(array, -reach, reach).astype(held_as)


def setup_inputs(seed: int = 0) -> dict:
    streams_of = jax.random.split(jax.random.key(seed), 12)
    hidden_in = scatter_about(streams_of[0], (TOKENS, MODEL_WIDTH), 1.0, 6.0, ((0, 32),))
    positions = draw_positions(jax.random.fold_in(streams_of[11], 71), 0)
    w_query = scatter_about(streams_of[2], (MODEL_WIDTH, QUERY_HEADS * HEAD_SIZE), MODEL_WIDTH ** -0.5, 0.1875, ((0, 16), (1, 2)))
    key_projection_weight = scatter_about(streams_of[3], (MODEL_WIDTH, KEY_VALUE_HEADS * HEAD_SIZE), MODEL_WIDTH ** -0.5, 0.1875, ((0, 16), (1, 2)))
    value_projection_weight = scatter_about(streams_of[4], (MODEL_WIDTH, KEY_VALUE_HEADS * HEAD_SIZE), MODEL_WIDTH ** -0.5, 0.1875, ((0, 16), (1, 2)))
    w_output = scatter_about(streams_of[5], (QUERY_HEADS * HEAD_SIZE, MODEL_WIDTH), (2 * HEAD_SIZE) ** -0.5, 0.375, ((0, 2), (1, 16)))
    w_gate = scatter_about(streams_of[6], (MODEL_WIDTH, FF), MODEL_WIDTH ** -0.5, 0.1875, ((0, 16), (1, 2)))
    w_up = scatter_about(streams_of[7], (MODEL_WIDTH, FF), MODEL_WIDTH ** -0.5, 0.1875, ((0, 16), (1, 2)))
    w_down = scatter_about(streams_of[8], (FF, MODEL_WIDTH), FF ** -0.5, 0.109375, ((0, 2), (1, 16)))
    norm_gains = draw_norm_gains(jax.random.fold_in(streams_of[11], 71), 0)
    grad_out = draw_grad_out(jax.random.fold_in(streams_of[11], 71), 0)
    return dict(hidden_in=hidden_in, positions=positions, w_query=w_query, key_projection_weight=key_projection_weight, value_projection_weight=value_projection_weight, w_output=w_output, w_gate=w_gate, w_up=w_up, w_down=w_down, norm_gains=norm_gains, grad_out=grad_out)


EPSILON = 1e-06
THETA = 1000000.0

def rms_scale(values, scales):
    return values * lax.rsqrt(lax.optimization_barrier(jnp.mean(values * values, axis=-1, keepdims=True)) + EPSILON) * scales

def rotate_half(values):
    middle = values.shape[-1] // 2
    return jnp.concatenate([-values[..., middle:], values[..., :middle]], axis=-1)

def rope_tables(position):
    frequency = jnp.exp(jnp.arange(HEAD_SIZE // 2, dtype=jnp.float32) * (-2.0 * math.log(THETA) / HEAD_SIZE))
    angles = position.astype(jnp.float32)[:, None] * frequency[None, :]
    cosine = jnp.concatenate([jnp.cos(angles), jnp.cos(angles)], axis=-1)
    sinusoid = jnp.concatenate([jnp.sin(angles), jnp.sin(angles)], axis=-1)
    return (cosine, sinusoid)

def head_piece(raw_heads, scales, cosine, sinusoid):
    normed = rms_scale(raw_heads, scales)
    return normed * cosine[:, None, :] + rotate_half(normed) * sinusoid[:, None, :]

def causal_mask(position):
    count_of_rows = position.shape[0]
    query_index = jnp.arange(count_of_rows, dtype=jnp.int32)[:, None]
    key_index = jnp.arange(count_of_rows, dtype=jnp.int32)[None, :]
    return (key_index <= query_index) & (key_index >= query_index - position[:, None])

def group_pass(matrices, gains, inputs, position, cotangent):
    w_query, key_projection_weight, value_projection_weight, w_output, w_gate, w_up, w_down = matrices
    count_of_rows = inputs.shape[0]
    heads_per_group = QUERY_HEADS // KEY_VALUE_HEADS
    scale = HEAD_SIZE ** (-0.5)
    gain_attn = gains[:MODEL_WIDTH]
    gain_ffn = gains[MODEL_WIDTH:2 * MODEL_WIDTH]
    gain_q = gains[2 * MODEL_WIDTH:2 * MODEL_WIDTH + HEAD_SIZE]
    gain_k = gains[2 * MODEL_WIDTH + HEAD_SIZE:]
    input_f = inputs.astype(jnp.float32)
    attention_normed = rms_scale(input_f, gain_attn).astype(jnp.bfloat16)
    q_raw = jnp.dot(attention_normed, w_query, preferred_element_type=jnp.float32).reshape(count_of_rows, QUERY_HEADS, HEAD_SIZE)
    raw_key_rows = jnp.dot(attention_normed, key_projection_weight, preferred_element_type=jnp.float32).reshape(count_of_rows, KEY_VALUE_HEADS, HEAD_SIZE)
    value_rows = jnp.dot(attention_normed, value_projection_weight, preferred_element_type=jnp.float32).astype(jnp.bfloat16).reshape(count_of_rows, KEY_VALUE_HEADS, HEAD_SIZE)
    cosine, sinusoid = rope_tables(position)
    rotated_query, query_back = jax.vjp(lambda raw_heads, scales: head_piece(raw_heads, scales, cosine, sinusoid), q_raw, gain_q)
    key_rot, key_back = jax.vjp(lambda raw_heads, scales: head_piece(raw_heads, scales, cosine, sinusoid), raw_key_rows, gain_k)
    query_rows = rotated_query.astype(jnp.bfloat16).reshape(count_of_rows, KEY_VALUE_HEADS, heads_per_group, HEAD_SIZE).astype(jnp.float32)
    key = key_rot.astype(jnp.bfloat16).astype(jnp.float32)
    value_f = value_rows.astype(jnp.float32)
    mask = causal_mask(position)
    scores = jnp.einsum('qhgd,khd->hgqk', query_rows, key) * scale
    masked = jnp.where(mask, scores, -1e+30)
    largest = lax.optimization_barrier(jnp.max(masked, axis=-1, keepdims=True))
    lse = largest + jnp.log(lax.optimization_barrier(jnp.sum(jnp.exp(masked - largest), axis=-1, keepdims=True)))
    probs = jnp.exp(masked - lse)
    float_probabilities = probs.astype(jnp.bfloat16).astype(jnp.float32)
    attended = jnp.einsum('hgqk,khd->qhgd', float_probabilities, value_f).astype(jnp.bfloat16)
    attended_flat = attended.reshape(count_of_rows, QUERY_HEADS * HEAD_SIZE)
    mid = input_f + jnp.dot(attended_flat, w_output, preferred_element_type=jnp.float32)
    normed_ffn = rms_scale(mid, gain_ffn).astype(jnp.bfloat16)
    gate_pre = jnp.dot(normed_ffn, w_gate, preferred_element_type=jnp.float32)
    up_pre = jnp.dot(normed_ffn, w_up, preferred_element_type=jnp.float32)
    mixed = (jax.nn.silu(gate_pre) * up_pre).astype(jnp.bfloat16)
    out_rows = (mid + jnp.dot(mixed, w_down, preferred_element_type=jnp.float32)).astype(jnp.bfloat16)
    grad_down = jnp.dot(mixed.T, cotangent, preferred_element_type=jnp.float32)
    grad_mixed = jnp.dot(cotangent, w_down.T, preferred_element_type=jnp.float32)
    sigmoid_gate = jax.nn.sigmoid(gate_pre)
    grad_gate_pre = (grad_mixed * up_pre * sigmoid_gate * (1.0 + gate_pre * (1.0 - sigmoid_gate))).astype(jnp.bfloat16)
    grad_up_pre = (grad_mixed * gate_pre * sigmoid_gate).astype(jnp.bfloat16)
    grad_gate = jnp.dot(normed_ffn.T, grad_gate_pre, preferred_element_type=jnp.float32)
    grad_up = jnp.dot(normed_ffn.T, grad_up_pre, preferred_element_type=jnp.float32)
    grad_normed_ffn = jnp.dot(grad_gate_pre, w_gate.T, preferred_element_type=jnp.float32) + jnp.dot(grad_up_pre, w_up.T, preferred_element_type=jnp.float32)
    grad_mid_norm, grad_gain_ffn = jax.vjp(rms_scale, mid, gain_ffn)[1](grad_normed_ffn)
    grad_mid = cotangent.astype(jnp.float32) + grad_mid_norm
    grad_mid_b = grad_mid.astype(jnp.bfloat16)
    grad_output = jnp.dot(attended_flat.T, grad_mid_b, preferred_element_type=jnp.float32)
    attended_gradient = jnp.dot(grad_mid_b, w_output.T, preferred_element_type=jnp.float32).astype(jnp.bfloat16)
    attended_gradient = attended_gradient.reshape(count_of_rows, KEY_VALUE_HEADS, heads_per_group, HEAD_SIZE).astype(jnp.float32)
    grad_probs = jnp.einsum('qhgd,khd->hgqk', attended_gradient, value_f)
    delta = jnp.einsum('qhgd,qhgd->hgq', attended_gradient, attended.astype(jnp.float32))[..., None]
    grad_scores = (probs * (grad_probs - delta) * scale).astype(jnp.bfloat16).astype(jnp.float32)
    grad_query_rot = jnp.einsum('hgqk,khd->qhgd', grad_scores, key).reshape(count_of_rows, QUERY_HEADS, HEAD_SIZE)
    grad_key_rot = jnp.einsum('bmvx,vbma->xba', grad_scores, query_rows)
    value_gradient = jnp.einsum('bmvx,vbma->xba', float_probabilities, attended_gradient).astype(jnp.bfloat16).reshape(count_of_rows, KEY_VALUE_HEADS * HEAD_SIZE)
    grad_q_raw, grad_gain_q = query_back(grad_query_rot)
    raw_key_gradient, grad_gain_k = key_back(grad_key_rot)
    grad_q_b = grad_q_raw.reshape(count_of_rows, QUERY_HEADS * HEAD_SIZE).astype(jnp.bfloat16)
    key_block_gradient = raw_key_gradient.reshape(count_of_rows, KEY_VALUE_HEADS * HEAD_SIZE).astype(jnp.bfloat16)
    grad_query = jnp.dot(attention_normed.T, grad_q_b, preferred_element_type=jnp.float32)
    grad_key = jnp.dot(attention_normed.T, key_block_gradient, preferred_element_type=jnp.float32)
    grad_value = jnp.dot(attention_normed.T, value_gradient, preferred_element_type=jnp.float32)
    grad_normed_attn = jnp.dot(grad_q_b, w_query.T, preferred_element_type=jnp.float32)
    grad_normed_attn = grad_normed_attn + jnp.dot(key_block_gradient, key_projection_weight.T, preferred_element_type=jnp.float32)
    grad_normed_attn = grad_normed_attn + jnp.dot(value_gradient, value_projection_weight.T, preferred_element_type=jnp.float32)
    grad_in_norm, grad_gain_attn = jax.vjp(rms_scale, input_f, gain_attn)[1](grad_normed_attn)
    grad_rows = (grad_mid + grad_in_norm).astype(jnp.bfloat16)
    gain_grad = jnp.concatenate([grad_gain_attn, grad_gain_ffn, grad_gain_q, grad_gain_k])
    grads = (grad_query, grad_key, grad_value, grad_output, grad_gate, grad_up, grad_down, gain_grad)
    return (out_rows, grad_rows, grads)

def reference(hidden_in, positions, w_query, key_projection_weight, value_projection_weight, w_output, w_gate, w_up, w_down, norm_gains, grad_out):
    group_count = TOKENS // GROUP
    matrices = (w_query, key_projection_weight, value_projection_weight, w_output, w_gate, w_up, w_down)
    initial = tuple((jnp.zeros(matrix.shape, jnp.float32) for matrix in matrices)) + (jnp.zeros(norm_gains.shape, jnp.float32),)

    def step(carry, block):
        inputs, position, cotangent = block
        out_rows, grad_rows, grads = group_pass(matrices, norm_gains, inputs, position, cotangent)
        carry = tuple((running + update for running, update in zip(carry, grads)))
        return (carry, (out_rows, grad_rows))
    blocks = (hidden_in.reshape(group_count, GROUP, MODEL_WIDTH), positions.reshape(group_count, GROUP), grad_out.reshape(group_count, GROUP, MODEL_WIDTH))
    sums, (outputs, gradients) = lax.scan(step, initial, blocks)
    return (outputs.reshape(TOKENS, MODEL_WIDTH), gradients.reshape(TOKENS, MODEL_WIDTH), sums[0], sums[1], sums[2], sums[3], sums[4], sums[5], sums[6], sums[7])
```

```python
import math

import jax
import jax.numpy as jnp
from jax import lax
from jax.sharding import PartitionSpec as P

HEAD_SIZE = 128
EPSILON = 1e-06
THETA = 1000000.0


def rms_scale(values, scales):
    return values * lax.rsqrt(jnp.mean(values * values, axis=-1, keepdims=True) + EPSILON) * scales


def rotate_half(values):
    middle = values.shape[-1] // 2
    return jnp.concatenate([-values[..., middle:], values[..., :middle]], axis=-1)


def rope_tables(position):
    frequency = jnp.exp(
        jnp.arange(HEAD_SIZE // 2, dtype=jnp.float32) * (-2.0 * math.log(THETA) / HEAD_SIZE)
    )
    angles = position.astype(jnp.float32)[:, None] * frequency[None, :]
    cosine = jnp.cos(angles)
    sinusoid = jnp.sin(angles)
    return (
        jnp.concatenate([cosine, cosine], axis=-1),
        jnp.concatenate([sinusoid, sinusoid], axis=-1),
    )


def head_piece(raw_heads, scales, cosine, sinusoid):
    normed = rms_scale(raw_heads, scales)
    return normed * cosine[:, None, :] + rotate_half(normed) * sinusoid[:, None, :]


def dot_f32(a, b):
    return jnp.dot(a, b, preferred_element_type=jnp.float32)


def dot_rows(a, b):
    return lax.dot_general(a, b, (((0,), (0,)), ((), ())), preferred_element_type=jnp.float32)


def dot_cols(a, b):
    return lax.dot_general(a, b, (((1,), (1,)), ((), ())), preferred_element_type=jnp.float32)


class Layout:
    def __init__(self, dp, tensor, team):
        self.dp, self.tensor, self.team, self.line = dp, tensor, team, dp // team
        index = lax.axis_index("dp")
        self.index = index
        self.z = index // team
        self.t = index % team
        self.core = lax.axis_index("tensor")

    def to_peer(self, value, r):
        team = self.team
        pairs = [(i, (i // team) * team + ((i % team) ^ r)) for i in range(self.dp)]
        return lax.ppermute(value, "dp", pairs)

    def to_core(self, value):
        return lax.ppermute(value, "tensor", [(0, 1), (1, 0)])

    def step(self, value, delta, zs):
        team = self.team
        pairs = [(z * team + t, (z + delta) * team + t) for z in zs for t in range(team)]
        return lax.ppermute(value, "dp", pairs)

    def xor_order(self, blocks):
        blocks = list(blocks)
        bit = 1
        while bit < self.team:
            odd = (self.t & bit) != 0
            blocks = [jnp.where(odd, blocks[r ^ bit], blocks[r]) for r in range(self.team)]
            bit *= 2
        return blocks

    def rotate(self, value, back=False):
        width = value.shape[-1]
        chunk = width // self.line
        start = (self.line - self.z) % self.line if back else self.z
        doubled = jnp.concatenate([value, value], axis=-1)
        return lax.dynamic_slice_in_dim(doubled, start * chunk, width, axis=value.ndim - 1)

    def gather_tokens(self, own):
        mine = [own] + [self.to_peer(own, r) for r in range(1, self.team)]
        other = [self.to_core(part) for part in mine]
        return jnp.concatenate(mine + other, axis=0)

    def scatter_tokens(self, product):
        team = self.team
        rows = self.rows
        half = team * rows
        theirs = self.to_core(product(half, 2 * half).astype(jnp.bfloat16))
        summed = product(0, half) + theirs.astype(jnp.float32)
        total = summed[:rows]
        for r in range(1, team):
            piece = summed[r * rows : (r + 1) * rows].astype(jnp.bfloat16)
            total = total + self.to_peer(piece, r).astype(jnp.float32)
        return total

    def trade_columns(self, blocks):
        relative = self.xor_order(blocks)
        got = [relative[0]] + [self.to_peer(relative[r], r) for r in range(1, self.team)]
        return jnp.concatenate(self.xor_order(got), axis=0)

    def line_gather(self, block):
        line = self.line
        if line > 8:
            groups = [[z * self.team + t for z in range(line)] for t in range(self.team)]
            full = lax.all_gather(block, "dp", axis=0, tiled=True, axis_index_groups=groups)
            doubled = jnp.concatenate([full, full], axis=0)
            return lax.dynamic_slice_in_dim(
                doubled, self.z * block.shape[0], full.shape[0], axis=0
            )
        lower = [block]
        upper = [block]
        for k in range(1, line):
            lower.append(self.step(lower[-1], 1, range(k - 1, line - 1)))
            upper.append(self.step(upper[-1], -1, range(1, line - k + 1)))
        parts = [block]
        for j in range(1, line):
            parts.append(jnp.where(self.z + j < line, upper[j], lower[line - j]))
        return jnp.concatenate(parts, axis=0)

    def line_scatter(self, grad):
        line = self.line
        chunk = grad.shape[0] // line
        if line > 8:
            groups = [[z * self.team + t for z in range(line)] for t in range(self.team)]
            doubled = jnp.concatenate([grad, grad], axis=0)
            start = ((line - self.z) % line) * chunk
            plain = lax.dynamic_slice_in_dim(doubled, start, grad.shape[0], axis=0)
            return lax.psum_scatter(
                plain.astype(jnp.bfloat16),
                "dp",
                scatter_dimension=0,
                tiled=True,
                axis_index_groups=groups,
            ).astype(jnp.float32)
        part = [grad[j * chunk : (j + 1) * chunk] for j in range(line)]
        up = down = None
        for k in range(1, line):
            rising = part[line - k] if up is None else part[line - k] + up.astype(jnp.float32)
            falling = part[k] if down is None else part[k] + down.astype(jnp.float32)
            up = self.step(rising.astype(jnp.bfloat16), 1, range(0, k))
            down = self.step(falling.astype(jnp.bfloat16), -1, range(line - k, line))
        total = part[0]
        if up is not None:
            total = total + up.astype(jnp.float32) + down.astype(jnp.float32)
        return total

    def return_columns(self, summed):
        rows = summed.shape[0] // self.team
        blocks = [summed[s * rows : (s + 1) * rows] for s in range(self.team)]
        relative = self.xor_order(blocks)
        got = [relative[0]]
        for r in range(1, self.team):
            got.append(
                self.to_peer(relative[r].astype(jnp.bfloat16), r).astype(jnp.float32)
            )
        return self.xor_order(got)

    def gather_small(self, value):
        if self.dp & (self.dp - 1):
            return lax.all_gather(value, "dp", axis=0, tiled=True)
        full = value[None, :]
        bit = 1
        while bit < self.dp:
            other = lax.ppermute(full, "dp", [(i, i ^ bit) for i in range(self.dp)])
            odd = (self.index & bit) != 0
            full = jnp.where(
                odd,
                jnp.concatenate([other, full], axis=0),
                jnp.concatenate([full, other], axis=0),
            )
            bit *= 2
        return full.reshape(-1)

    def sum_small(self, value):
        if self.dp & (self.dp - 1):
            return lax.psum(value, ("dp", "tensor"))
        value = value + self.to_core(value)
        bit = 1
        while bit < self.dp:
            value = value + lax.ppermute(value, "dp", [(i, i ^ bit) for i in range(self.dp)])
            bit *= 2
        return value


def split_columns(weight, team):
    width = weight.shape[1] // team
    return [weight[:, s * width : (s + 1) * width] for s in range(team)]


def make_body(dp, tensor):
    def per_device(
        hidden_in,
        positions,
        w_query,
        w_key,
        w_value,
        w_output,
        w_gate,
        w_up,
        w_down,
        norm_gains,
        grad_out,
    ):
        scale = HEAD_SIZE ** (-0.5)
        rows, width = hidden_in.shape
        group = positions.shape[0]
        team = math.gcd(dp, w_key.shape[1] // HEAD_SIZE)
        lay = Layout(dp, tensor, team)
        lay.rows = rows
        heads_kv = w_key.shape[1] // HEAD_SIZE // team
        heads_q = w_query.shape[1] // HEAD_SIZE // team
        per_kv = heads_q // heads_kv
        q_cols, kv_cols = heads_q * HEAD_SIZE, heads_kv * HEAD_SIZE
        ff = w_gate.shape[1] // team
        tokens = team * group

        def merge(*weights):
            pieces = [split_columns(w, team) for w in weights]
            return [jnp.concatenate([p[s] for p in pieces], axis=1) for s in range(team)]

        attn_block = lay.trade_columns(merge(w_query, w_key, w_value))
        hidden_own = lay.rotate(hidden_in)
        inputs = lay.gather_tokens(hidden_own)
        gains = lay.gather_small(norm_gains)
        seats = [positions] + [lay.to_peer(positions, r) for r in range(1, team)]
        attn_w = lay.line_gather(attn_block)
        out_w = lay.line_gather(lay.trade_columns(merge(w_output.T)))
        ffn_w = lay.line_gather(lay.trade_columns(merge(w_gate, w_up)))
        down_w = lay.line_gather(lay.trade_columns(merge(w_down.T)))
        cot_own = lay.rotate(grad_out)
        cot = lay.gather_tokens(cot_own)

        gain_attn = lay.rotate(gains[:width])
        gain_ffn = lay.rotate(gains[width : 2 * width])
        gain_q = gains[2 * width : 2 * width + HEAD_SIZE]
        gain_k = gains[2 * width + HEAD_SIZE :]

        def own_first(group_values):
            low, high = group_values[:rows], group_values[rows:]
            first = lay.core == 0
            return jnp.where(first, low, high), jnp.where(first, high, low)

        seat_pairs = [own_first(s) for s in seats]
        place_mine, place_other = own_first(jnp.arange(group, dtype=jnp.int32))
        place = jnp.concatenate([place_mine, place_other])
        seat_groups = jnp.stack([jnp.concatenate(pair) for pair in seat_pairs])
        seat_tokens = jnp.concatenate(
            [pair[0] for pair in seat_pairs] + [pair[1] for pair in seat_pairs]
        )
        query_place = place[None, :, None]
        key_place = place[None, None, :]
        mask = (key_place <= query_place) & (key_place >= query_place - seat_groups[:, :, None])
        mask = mask[:, None, None]
        cosine, sinusoid = rope_tables(seat_tokens)

        def to_groups(v, heads):
            v = v.reshape(2, team, rows, heads, HEAD_SIZE)
            return v.transpose(1, 3, 0, 2, 4).reshape(team, heads, group, HEAD_SIZE)

        def to_tokens(v, heads):
            v = v.reshape(team, heads, 2, rows, HEAD_SIZE)
            return v.transpose(2, 0, 3, 1, 4).reshape(tokens, heads, HEAD_SIZE)

        normed = rms_scale(inputs.astype(jnp.float32), gain_attn).astype(jnp.bfloat16)
        raw = dot_f32(normed, attn_w)
        q_raw = raw[:, :q_cols].reshape(tokens, heads_q, HEAD_SIZE)
        k_raw = raw[:, q_cols : q_cols + kv_cols].reshape(tokens, heads_kv, HEAD_SIZE)
        value = raw[:, q_cols + kv_cols :].astype(jnp.bfloat16)
        value = to_groups(value, heads_kv)

        def rotary(raw_heads, scales):
            return head_piece(raw_heads, scales, cosine, sinusoid)

        query_rot, query_back = jax.vjp(rotary, q_raw, gain_q)
        key_rot, key_back = jax.vjp(rotary, k_raw, gain_k)
        query = to_groups(query_rot.astype(jnp.bfloat16), heads_q)
        query = query.reshape(team, heads_kv, per_kv, group, HEAD_SIZE)
        key = to_groups(key_rot.astype(jnp.bfloat16), heads_kv)

        scores = (
            jnp.einsum("thgqd,thkd->thgqk", query, key, preferred_element_type=jnp.float32) * scale
        )
        masked = jnp.where(mask, scores, -1e30)
        largest = jnp.max(masked, axis=-1, keepdims=True)
        lse = largest + jnp.log(jnp.sum(jnp.exp(masked - largest), axis=-1, keepdims=True))
        probs = jnp.exp(masked - lse)
        probs_b = probs.astype(jnp.bfloat16)
        attended = jnp.einsum(
            "thgqk,thkd->thgqd", probs_b, value, preferred_element_type=jnp.float32
        ).astype(jnp.bfloat16)
        attended_flat = to_tokens(
            attended.reshape(team, heads_q, group, HEAD_SIZE), heads_q
        ).reshape(tokens, q_cols)

        mid = hidden_own.astype(jnp.float32) + lay.scatter_tokens(
            lambda lo, hi: dot_cols(attended_flat[lo:hi], out_w)
        )
        normed_own, ffn_back = jax.vjp(rms_scale, mid, gain_ffn)
        ffn_in = lay.gather_tokens(normed_own.astype(jnp.bfloat16))
        both = dot_f32(ffn_in, ffn_w)
        gate_pre, up_pre = both[:, :ff], both[:, ff:]
        sigmoid_gate = jax.nn.sigmoid(gate_pre)
        mixed = (gate_pre * sigmoid_gate * up_pre).astype(jnp.bfloat16)
        grad_mixed = dot_f32(cot, down_w)
        grad_gate_pre = (
            grad_mixed * up_pre * sigmoid_gate * (1.0 + gate_pre * (1.0 - sigmoid_gate))
        ).astype(jnp.bfloat16)
        grad_up_pre = (grad_mixed * gate_pre * sigmoid_gate).astype(jnp.bfloat16)
        grad_both = jnp.concatenate([grad_gate_pre, grad_up_pre], axis=1)
        grad_normed_ffn = lay.scatter_tokens(lambda lo, hi: dot_cols(grad_both[lo:hi], ffn_w))
        grad_mid_norm, grad_gain_ffn = ffn_back(grad_normed_ffn)
        grad_mid = cot_own.astype(jnp.float32) + grad_mid_norm
        grad_mid_all = lay.gather_tokens(grad_mid.astype(jnp.bfloat16))

        grad_down = lay.return_columns(lay.line_scatter(dot_rows(cot, mixed)))
        grad_ffn = lay.return_columns(lay.line_scatter(dot_rows(ffn_in, grad_both)))
        hidden_out = (
            mid + lay.scatter_tokens(lambda lo, hi: dot_cols(mixed[lo:hi], down_w))
        ).astype(jnp.bfloat16)

        grad_att = dot_f32(grad_mid_all, out_w).astype(jnp.bfloat16)
        grad_att = to_groups(grad_att, heads_q).reshape(team, heads_kv, per_kv, group, HEAD_SIZE)
        grad_o = lay.return_columns(lay.line_scatter(dot_rows(grad_mid_all, attended_flat)))
        grad_probs = jnp.einsum(
            "thgqd,thkd->thgqk", grad_att, value, preferred_element_type=jnp.float32
        )
        delta = jnp.sum(
            grad_att.astype(jnp.float32) * attended.astype(jnp.float32), axis=-1, keepdims=True
        )
        grad_scores = (probs * (grad_probs - delta) * scale).astype(jnp.bfloat16)
        grad_query_rot = jnp.einsum(
            "thgqk,thkd->thgqd", grad_scores, key, preferred_element_type=jnp.float32
        ).reshape(team, heads_q, group, HEAD_SIZE)
        grad_key_rot = jnp.einsum(
            "thgqk,thgqd->thkd", grad_scores, query, preferred_element_type=jnp.float32
        )
        grad_v = jnp.einsum(
            "thgqk,thgqd->thkd", probs_b, grad_att, preferred_element_type=jnp.float32
        ).astype(jnp.bfloat16)
        grad_q_raw, grad_gain_q = query_back(to_tokens(grad_query_rot, heads_q))
        grad_k_raw, grad_gain_k = key_back(to_tokens(grad_key_rot, heads_kv))
        grad_qkv = jnp.concatenate(
            [
                grad_q_raw.reshape(tokens, q_cols).astype(jnp.bfloat16),
                grad_k_raw.reshape(tokens, kv_cols).astype(jnp.bfloat16),
                to_tokens(grad_v, heads_kv).reshape(tokens, kv_cols),
            ],
            axis=1,
        )
        grad_qkv_w = lay.return_columns(lay.line_scatter(dot_rows(normed, grad_qkv)))
        grad_normed_attn = lay.scatter_tokens(lambda lo, hi: dot_cols(grad_qkv[lo:hi], attn_w))
        _, attn_back = jax.vjp(rms_scale, hidden_own.astype(jnp.float32), gain_attn)
        grad_in_norm, grad_gain_attn = attn_back(grad_normed_attn)
        grad_in = (grad_mid + grad_in_norm).astype(jnp.bfloat16)

        gain_parts = jnp.concatenate(
            [
                lay.rotate(grad_gain_attn, back=True),
                lay.rotate(grad_gain_ffn, back=True),
                grad_gain_q,
                grad_gain_k,
            ]
        )
        gain_total = lay.sum_small(gain_parts)
        share = gain_total.shape[0] // (dp * tensor)
        seat = lay.index * tensor + lay.core
        grad_gains = lax.dynamic_slice_in_dim(gain_total, seat * share, share, axis=0)

        def columns(blocks, lo, hi):
            return jnp.concatenate([b[:, lo:hi] for b in blocks], axis=1)

        return (
            lay.rotate(hidden_out, back=True),
            lay.rotate(grad_in, back=True),
            columns(grad_qkv_w, 0, q_cols),
            columns(grad_qkv_w, q_cols, q_cols + kv_cols),
            columns(grad_qkv_w, q_cols + kv_cols, q_cols + 2 * kv_cols),
            columns(grad_o, 0, q_cols).T,
            columns(grad_ffn, 0, ff),
            columns(grad_ffn, ff, 2 * ff),
            columns(grad_down, 0, ff).T,
            grad_gains,
        )

    return per_device


def solution(mesh):
    placed = (
        P(("dp", "tensor"), None),
        P("dp"),
        P("dp", "tensor"),
        P("dp", "tensor"),
        P("dp", "tensor"),
        P("tensor", "dp"),
        P("dp", "tensor"),
        P("dp", "tensor"),
        P("tensor", "dp"),
        P("dp"),
        P(("dp", "tensor"), None),
    )
    return jax.shard_map(
        make_body(mesh.shape["dp"], mesh.shape["tensor"]),
        mesh=mesh,
        in_specs=placed,
        out_specs=(
            P(("dp", "tensor"), None),
            P(("dp", "tensor"), None),
            P("dp", "tensor"),
            P("dp", "tensor"),
            P("dp", "tensor"),
            P("tensor", "dp"),
            P("dp", "tensor"),
            P("dp", "tensor"),
            P("tensor", "dp"),
            P(("dp", "tensor")),
        ),
        check_vma=False,
    )
```

```python
import math

import jax
import jax.numpy as jnp
from jax import lax
from jax.sharding import PartitionSpec as P

HEAD_SIZE = 128
EPSILON = 1e-06
THETA = 1000000.0


def rms_scale(values, scales):
    return values * lax.rsqrt(jnp.mean(values * values, axis=-1, keepdims=True) + EPSILON) * scales


def rotate_half(values):
    middle = values.shape[-1] // 2
    return jnp.concatenate([-values[..., middle:], values[..., :middle]], axis=-1)


def rope_tables(position):
    frequency = jnp.exp(
        jnp.arange(HEAD_SIZE // 2, dtype=jnp.float32) * (-2.0 * math.log(THETA) / HEAD_SIZE)
    )
    angles = position.astype(jnp.float32)[:, None] * frequency[None, :]
    cosine = jnp.cos(angles)
    sinusoid = jnp.sin(angles)
    return (
        jnp.concatenate([cosine, cosine], axis=-1),
        jnp.concatenate([sinusoid, sinusoid], axis=-1),
    )


def head_piece(raw_heads, scales, cosine, sinusoid):
    normed = rms_scale(raw_heads, scales)
    return normed * cosine[:, None, :] + rotate_half(normed) * sinusoid[:, None, :]


def dot_f32(a, b):
    return jnp.dot(a, b, preferred_element_type=jnp.float32)


def dot_rows(a, b):
    return lax.dot_general(a, b, (((0,), (0,)), ((), ())), preferred_element_type=jnp.float32)


def dot_cols(a, b):
    return lax.dot_general(a, b, (((1,), (1,)), ((), ())), preferred_element_type=jnp.float32)


class Layout:
    def __init__(self, dp, tensor, team):
        self.dp, self.tensor, self.team, self.line = dp, tensor, team, dp // team
        index = lax.axis_index("dp")
        self.index = index
        self.z = index // team
        self.t = index % team
        self.core = lax.axis_index("tensor")

    def to_peer(self, value, r):
        team = self.team
        pairs = [(i, (i // team) * team + ((i % team) ^ r)) for i in range(self.dp)]
        return lax.ppermute(value, "dp", pairs)

    def to_core(self, value):
        return lax.ppermute(value, "tensor", [(0, 1), (1, 0)])

    def xor_order(self, blocks):
        blocks = list(blocks)
        bit = 1
        while bit < self.team:
            odd = (self.t & bit) != 0
            blocks = [jnp.where(odd, blocks[r ^ bit], blocks[r]) for r in range(self.team)]
            bit *= 2
        return blocks

    def gather_tokens(self, own):
        mine = [own] + [self.to_peer(own, r) for r in range(1, self.team)]
        other = [self.to_core(part) for part in mine]
        return jnp.concatenate(mine + other, axis=0)

    def scatter_tokens(self, product):
        team = self.team
        rows = self.rows
        half = team * rows
        theirs = self.to_core(product(half, 2 * half).astype(jnp.bfloat16))
        summed = product(0, half) + theirs.astype(jnp.float32)
        total = summed[:rows]
        for r in range(1, team):
            piece = summed[r * rows : (r + 1) * rows].astype(jnp.bfloat16)
            total = total + self.to_peer(piece, r).astype(jnp.float32)
        return total

    def trade_columns(self, blocks):
        relative = self.xor_order(blocks)
        got = [relative[0]] + [self.to_peer(relative[r], r) for r in range(1, self.team)]
        return jnp.concatenate(self.xor_order(got), axis=0)

    def lines(self):
        return [[z * self.team + t for z in range(self.line)] for t in range(self.team)]

    def line_gather(self, block):
        return lax.all_gather(block, "dp", axis=0, tiled=True, axis_index_groups=self.lines())

    def line_scatter(self, grad):
        return lax.psum_scatter(
            grad.astype(jnp.bfloat16),
            "dp",
            scatter_dimension=0,
            tiled=True,
            axis_index_groups=self.lines(),
        ).astype(jnp.float32)

    def return_columns(self, summed):
        rows = summed.shape[0] // self.team
        blocks = [summed[s * rows : (s + 1) * rows] for s in range(self.team)]
        relative = self.xor_order(blocks)
        got = [relative[0]]
        for r in range(1, self.team):
            got.append(
                self.to_peer(relative[r].astype(jnp.bfloat16), r).astype(jnp.float32)
            )
        return self.xor_order(got)

    def gather_small(self, value):
        if self.dp & (self.dp - 1):
            return lax.all_gather(value[None, :], "dp", axis=0, tiled=True)
        full = value[None, :]
        bit = 1
        while bit < self.dp:
            other = lax.ppermute(full, "dp", [(i, i ^ bit) for i in range(self.dp)])
            odd = (self.index & bit) != 0
            full = jnp.where(
                odd,
                jnp.concatenate([other, full], axis=0),
                jnp.concatenate([full, other], axis=0),
            )
            bit *= 2
        return full

    def sum_small(self, value):
        if self.dp & (self.dp - 1):
            return lax.psum(value, ("dp", "tensor"))
        value = value + self.to_core(value)
        bit = 1
        while bit < self.dp:
            value = value + lax.ppermute(value, "dp", [(i, i ^ bit) for i in range(self.dp)])
            bit *= 2
        return value


def split_columns(weight, team):
    width = weight.shape[1] // team
    return [weight[:, s * width : (s + 1) * width] for s in range(team)]


def make_body(dp, tensor):
    def per_device(
        hidden_in,
        positions,
        w_query,
        w_key,
        w_value,
        w_output,
        w_gate,
        w_up,
        w_down,
        norm_gains,
        grad_out,
    ):
        scale = HEAD_SIZE ** (-0.5)
        rows, width = hidden_in.shape
        group = positions.shape[0]
        team = math.gcd(dp, w_key.shape[1] // HEAD_SIZE)
        lay = Layout(dp, tensor, team)
        lay.rows = rows
        heads_kv = w_key.shape[1] // HEAD_SIZE // team
        heads_q = w_query.shape[1] // HEAD_SIZE // team
        per_kv = heads_q // heads_kv
        q_cols, kv_cols = heads_q * HEAD_SIZE, heads_kv * HEAD_SIZE
        ff = w_gate.shape[1] // team
        tokens = team * group

        def merge(*weights):
            pieces = [split_columns(w, team) for w in weights]
            return [jnp.concatenate([p[s] for p in pieces], axis=1) for s in range(team)]

        attn_block = lay.trade_columns(merge(w_query, w_key, w_value, w_output.T))
        attn_w = lay.line_gather(attn_block)
        out_w = attn_w[:, q_cols + 2 * kv_cols :]
        attn_w = attn_w[:, : q_cols + 2 * kv_cols]
        inputs = lay.gather_tokens(hidden_in)
        small = lay.gather_small(
            jnp.concatenate([norm_gains, positions.astype(jnp.float32)])
        )
        gains = small[:, : norm_gains.shape[0]].reshape(-1)
        team_seats = lax.dynamic_slice_in_dim(
            small[:, norm_gains.shape[0] :], lay.z * team, team, axis=0
        ).astype(jnp.int32)
        seats = lay.xor_order([team_seats[s] for s in range(team)])
        ffn_block = lay.trade_columns(merge(w_gate, w_up, w_down.T))
        ffn_w = lay.line_gather(ffn_block)
        down_w = ffn_w[:, 2 * ff :]
        ffn_w = ffn_w[:, : 2 * ff]
        cot = lay.gather_tokens(grad_out)

        gain_attn = gains[:width]
        gain_ffn = gains[width : 2 * width]
        gain_q = gains[2 * width : 2 * width + HEAD_SIZE]
        gain_k = gains[2 * width + HEAD_SIZE :]

        def own_first(group_values):
            low, high = group_values[:rows], group_values[rows:]
            first = lay.core == 0
            return jnp.where(first, low, high), jnp.where(first, high, low)

        seat_pairs = [own_first(s) for s in seats]
        place_mine, place_other = own_first(jnp.arange(group, dtype=jnp.int32))
        place = jnp.concatenate([place_mine, place_other])
        seat_groups = jnp.stack([jnp.concatenate(pair) for pair in seat_pairs])
        seat_tokens = jnp.concatenate(
            [pair[0] for pair in seat_pairs] + [pair[1] for pair in seat_pairs]
        )
        query_place = place[None, :, None]
        key_place = place[None, None, :]
        mask = (key_place <= query_place) & (key_place >= query_place - seat_groups[:, :, None])
        mask = mask[:, None, None]
        cosine, sinusoid = rope_tables(seat_tokens)

        def to_groups(v, heads):
            v = v.reshape(2, team, rows, heads, HEAD_SIZE)
            return v.transpose(1, 3, 0, 2, 4).reshape(team, heads, group, HEAD_SIZE)

        def to_tokens(v, heads):
            v = v.reshape(team, heads, 2, rows, HEAD_SIZE)
            return v.transpose(2, 0, 3, 1, 4).reshape(tokens, heads, HEAD_SIZE)

        normed = rms_scale(inputs.astype(jnp.float32), gain_attn).astype(jnp.bfloat16)
        raw = dot_f32(normed, attn_w)
        q_raw = raw[:, :q_cols].reshape(tokens, heads_q, HEAD_SIZE)
        k_raw = raw[:, q_cols : q_cols + kv_cols].reshape(tokens, heads_kv, HEAD_SIZE)
        value = raw[:, q_cols + kv_cols :].astype(jnp.bfloat16)
        value = to_groups(value, heads_kv)

        def rotary(raw_heads, scales):
            return head_piece(raw_heads, scales, cosine, sinusoid)

        query_rot, query_back = jax.vjp(rotary, q_raw, gain_q)
        key_rot, key_back = jax.vjp(rotary, k_raw, gain_k)
        query = to_groups(query_rot.astype(jnp.bfloat16), heads_q)
        query = query.reshape(team, heads_kv, per_kv, group, HEAD_SIZE)
        key = to_groups(key_rot.astype(jnp.bfloat16), heads_kv)

        scores = (
            jnp.einsum("thgqd,thkd->thgqk", query, key, preferred_element_type=jnp.float32) * scale
        )
        masked = jnp.where(mask, scores, -1e30)
        largest = jnp.max(masked, axis=-1, keepdims=True)
        lse = largest + jnp.log(jnp.sum(jnp.exp(masked - largest), axis=-1, keepdims=True))
        probs = jnp.exp(masked - lse)
        probs_b = probs.astype(jnp.bfloat16)
        attended = jnp.einsum(
            "thgqk,thkd->thgqd", probs_b, value, preferred_element_type=jnp.float32
        ).astype(jnp.bfloat16)
        attended_flat = to_tokens(
            attended.reshape(team, heads_q, group, HEAD_SIZE), heads_q
        ).reshape(tokens, q_cols)

        mid = hidden_in.astype(jnp.float32) + lay.scatter_tokens(
            lambda lo, hi: dot_cols(attended_flat[lo:hi], out_w)
        )
        normed_own, ffn_back = jax.vjp(rms_scale, mid, gain_ffn)
        ffn_in = lay.gather_tokens(normed_own.astype(jnp.bfloat16))
        both = dot_f32(ffn_in, ffn_w)
        gate_pre, up_pre = both[:, :ff], both[:, ff:]
        sigmoid_gate = jax.nn.sigmoid(gate_pre)
        mixed = (gate_pre * sigmoid_gate * up_pre).astype(jnp.bfloat16)
        grad_mixed = dot_f32(cot, down_w)
        grad_gate_pre = (
            grad_mixed * up_pre * sigmoid_gate * (1.0 + gate_pre * (1.0 - sigmoid_gate))
        ).astype(jnp.bfloat16)
        grad_up_pre = (grad_mixed * gate_pre * sigmoid_gate).astype(jnp.bfloat16)
        grad_both = jnp.concatenate([grad_gate_pre, grad_up_pre], axis=1)
        grad_normed_ffn = lay.scatter_tokens(lambda lo, hi: dot_cols(grad_both[lo:hi], ffn_w))
        grad_mid_norm, grad_gain_ffn = ffn_back(grad_normed_ffn)
        grad_mid = grad_out.astype(jnp.float32) + grad_mid_norm
        grad_mid_all = lay.gather_tokens(grad_mid.astype(jnp.bfloat16))

        grad_ffn = lay.return_columns(
            lay.line_scatter(
                jnp.concatenate([dot_rows(ffn_in, grad_both), dot_rows(cot, mixed)], axis=1)
            )
        )
        hidden_out = (
            mid + lay.scatter_tokens(lambda lo, hi: dot_cols(mixed[lo:hi], down_w))
        ).astype(jnp.bfloat16)

        grad_att = dot_f32(grad_mid_all, out_w).astype(jnp.bfloat16)
        grad_att = to_groups(grad_att, heads_q).reshape(team, heads_kv, per_kv, group, HEAD_SIZE)
        grad_probs = jnp.einsum(
            "thgqd,thkd->thgqk", grad_att, value, preferred_element_type=jnp.float32
        )
        delta = jnp.sum(
            grad_att.astype(jnp.float32) * attended.astype(jnp.float32), axis=-1, keepdims=True
        )
        grad_scores = (probs * (grad_probs - delta) * scale).astype(jnp.bfloat16)
        grad_query_rot = jnp.einsum(
            "thgqk,thkd->thgqd", grad_scores, key, preferred_element_type=jnp.float32
        ).reshape(team, heads_q, group, HEAD_SIZE)
        grad_key_rot = jnp.einsum(
            "thgqk,thgqd->thkd", grad_scores, query, preferred_element_type=jnp.float32
        )
        grad_v = jnp.einsum(
            "thgqk,thgqd->thkd", probs_b, grad_att, preferred_element_type=jnp.float32
        ).astype(jnp.bfloat16)
        grad_q_raw, grad_gain_q = query_back(to_tokens(grad_query_rot, heads_q))
        grad_k_raw, grad_gain_k = key_back(to_tokens(grad_key_rot, heads_kv))
        grad_qkv = jnp.concatenate(
            [
                grad_q_raw.reshape(tokens, q_cols).astype(jnp.bfloat16),
                grad_k_raw.reshape(tokens, kv_cols).astype(jnp.bfloat16),
                to_tokens(grad_v, heads_kv).reshape(tokens, kv_cols),
            ],
            axis=1,
        )
        grad_qkv_w = lay.return_columns(
            lay.line_scatter(
                jnp.concatenate(
                    [dot_rows(normed, grad_qkv), dot_rows(grad_mid_all, attended_flat)], axis=1
                )
            )
        )
        grad_normed_attn = lay.scatter_tokens(lambda lo, hi: dot_cols(grad_qkv[lo:hi], attn_w))
        _, attn_back = jax.vjp(rms_scale, hidden_in.astype(jnp.float32), gain_attn)
        grad_in_norm, grad_gain_attn = attn_back(grad_normed_attn)
        grad_in = (grad_mid + grad_in_norm).astype(jnp.bfloat16)

        gain_parts = jnp.concatenate(
            [
                grad_gain_attn,
                grad_gain_ffn,
                grad_gain_q,
                grad_gain_k,
            ]
        )
        gain_total = lay.sum_small(gain_parts)
        share = gain_total.shape[0] // (dp * tensor)
        seat = lay.index * tensor + lay.core
        grad_gains = lax.dynamic_slice_in_dim(gain_total, seat * share, share, axis=0)

        def columns(blocks, lo, hi):
            return jnp.concatenate([b[:, lo:hi] for b in blocks], axis=1)

        return (
            hidden_out,
            grad_in,
            columns(grad_qkv_w, 0, q_cols),
            columns(grad_qkv_w, q_cols, q_cols + kv_cols),
            columns(grad_qkv_w, q_cols + kv_cols, q_cols + 2 * kv_cols),
            columns(grad_qkv_w, q_cols + 2 * kv_cols, 2 * q_cols + 2 * kv_cols).T,
            columns(grad_ffn, 0, ff),
            columns(grad_ffn, ff, 2 * ff),
            columns(grad_ffn, 2 * ff, 3 * ff).T,
            grad_gains,
        )

    return per_device


def solution(mesh):
    placed = (
        P(("dp", "tensor"), None),
        P("dp"),
        P("dp", "tensor"),
        P("dp", "tensor"),
        P("dp", "tensor"),
        P("tensor", "dp"),
        P("dp", "tensor"),
        P("dp", "tensor"),
        P("tensor", "dp"),
        P("dp"),
        P(("dp", "tensor"), None),
    )
    return jax.shard_map(
        make_body(mesh.shape["dp"], mesh.shape["tensor"]),
        mesh=mesh,
        in_specs=placed,
        out_specs=(
            P(("dp", "tensor"), None),
            P(("dp", "tensor"), None),
            P("dp", "tensor"),
            P("dp", "tensor"),
            P("dp", "tensor"),
            P("tensor", "dp"),
            P("dp", "tensor"),
            P("dp", "tensor"),
            P("tensor", "dp"),
            P(("dp", "tensor")),
        ),
        check_vma=False,
    )
```

```python
import math

import jax
import jax.numpy as jnp
from jax import lax
from jax.experimental import pallas as pl
from jax.experimental.pallas import tpu as pltpu
from jax.sharding import PartitionSpec as P

HEAD_SIZE = 128
EPSILON = 1e-06
THETA = 1000000.0


def rms_scale(values, scales):
    return values * lax.rsqrt(jnp.mean(values * values, axis=-1, keepdims=True) + EPSILON) * scales


def rope_tables(position):
    frequency = jnp.exp(
        jnp.arange(HEAD_SIZE // 2, dtype=jnp.float32) * (-2.0 * math.log(THETA) / HEAD_SIZE)
    )
    angles = position.astype(jnp.float32)[:, None] * frequency[None, :]
    cosine = jnp.cos(angles)
    sinusoid = jnp.sin(angles)
    return (
        jnp.concatenate([cosine, cosine], axis=-1),
        jnp.concatenate([-sinusoid, sinusoid], axis=-1),
    )


def call(body, outs, args):
    vmem = pl.BlockSpec(memory_space=pltpu.VMEM)
    return pl.pallas_call(
        body,
        out_shape=[jax.ShapeDtypeStruct(shape, kind) for shape, kind in outs],
        in_specs=[vmem] * len(args),
        out_specs=[vmem] * len(outs),
    )(*args)


def nn(a, b):
    return lax.dot_general(a, b, (((1,), (0,)), ((), ())), preferred_element_type=jnp.float32)


def nt(a, b):
    return lax.dot_general(a, b, (((1,), (1,)), ((), ())), preferred_element_type=jnp.float32)


def tn(a, b):
    return lax.dot_general(a, b, (((0,), (0,)), ((), ())), preferred_element_type=jnp.float32)


def head(h):
    return slice(h * HEAD_SIZE, (h + 1) * HEAD_SIZE)


def inverse_rms(values):
    return lax.rsqrt(jnp.mean(values * values, axis=-1, keepdims=True) + EPSILON)


def attention_forward(blocks, weight, gain_attn, gain_q, gain_k, cosine, sinusoid, hidden, sizes):
    team, rows, heads_q, heads_kv = sizes
    width = weight.shape[0]
    q_cols, kv_cols = heads_q * HEAD_SIZE, heads_kv * HEAD_SIZE
    per_kv = heads_q // heads_kv
    half, group = team * rows, 2 * rows
    scale = HEAD_SIZE ** (-0.5)

    def body(*refs):
        x = refs[: 2 * team]
        w_ref, ga_ref, gq_ref, gk_ref, cos_ref, sin_ref, hide_ref = refs[2 * team : 2 * team + 7]
        normed_ref, raw_ref, qk_ref, v_ref, p_ref, att_ref, mine_ref, other_ref = refs[
            2 * team + 7 :
        ]
        for r in range(team):
            low = slice(r * rows, (r + 1) * rows)
            high = slice(half + r * rows, half + (r + 1) * rows)
            span = slice(r * group, (r + 1) * group)
            xs = jnp.concatenate([x[r][...], x[team + r][...]], axis=0).astype(jnp.float32)
            normed = (xs * inverse_rms(xs) * ga_ref[...]).astype(jnp.bfloat16)
            normed_ref[low, :] = normed[:rows]
            normed_ref[high, :] = normed[rows:]
            raw = nn(normed, w_ref[:, : q_cols + 2 * kv_cols])
            raw_ref[span, :] = raw[:, : q_cols + kv_cols]
            value = raw[:, q_cols + kv_cols :].astype(jnp.bfloat16)
            v_ref[span, :] = value
            cos, sin = cos_ref[span, :], sin_ref[span, :]
            rotated = []
            for h in range(heads_q + heads_kv):
                piece = raw[:, head(h)]
                gain = gq_ref[...] if h < heads_q else gk_ref[...]
                piece = piece * inverse_rms(piece) * gain
                piece = piece * cos + pltpu.roll(piece, HEAD_SIZE // 2, 1) * sin
                piece = piece.astype(jnp.bfloat16)
                qk_ref[span, head(h)] = piece
                rotated.append(piece)
            hide = hide_ref[span, :]
            parts = []
            for h in range(heads_q):
                key = rotated[heads_q + h // per_kv]
                scores = nt(rotated[h], key) * scale
                scores = jnp.where(hide < 0.0, -1e30, scores)
                largest = jnp.max(scores, axis=-1, keepdims=True)
                raised = jnp.exp(scores - largest)
                probs = raised / jnp.sum(raised, axis=-1, keepdims=True)
                at = (r * heads_q + h) * group
                p_ref[at : at + group, :] = probs
                parts.append(
                    nn(probs.astype(jnp.bfloat16), value[:, head(h // per_kv)]).astype(
                        jnp.bfloat16
                    )
                )
            attended = jnp.concatenate(parts, axis=1)
            att_ref[low, :] = attended[:rows]
            att_ref[high, :] = attended[rows:]
            product = nt(attended, w_ref[:, q_cols + 2 * kv_cols :])
            mine_ref[low, :] = product[:rows]
            other_ref[low, :] = product[rows:].astype(jnp.bfloat16)

    tokens = team * group
    outs = [
        ((tokens, width), jnp.bfloat16),
        ((tokens, q_cols + kv_cols), jnp.float32),
        ((tokens, q_cols + kv_cols), jnp.bfloat16),
        ((tokens, kv_cols), jnp.bfloat16),
        ((tokens * heads_q, group), jnp.float32),
        ((tokens, q_cols), jnp.bfloat16),
        ((half, width), jnp.float32),
        ((half, width), jnp.bfloat16),
    ]
    args = (*blocks, weight, gain_attn, gain_q, gain_k, cosine, sinusoid, hidden)
    return call(body, outs, args)


def ffn_both(blocks, cot_blocks, weight, team, rows):
    width = weight.shape[0]
    ff = weight.shape[1] // 3
    half, tokens = team * rows, 2 * team * rows

    def body(*refs):
        f, c = refs[: 2 * team], refs[2 * team : 4 * team]
        w_ref = refs[4 * team]
        all_ref, mixed_ref, grad_ref, mine_ref, other_ref = refs[4 * team + 1 :]
        for r in range(team):
            low = slice(r * rows, (r + 1) * rows)
            high = slice(half + r * rows, half + (r + 1) * rows)
            own = jnp.concatenate([f[r][...], f[team + r][...]], axis=0)
            all_ref[low, :] = own[:rows]
            all_ref[high, :] = own[rows:]
            cot = jnp.concatenate([c[r][...], c[team + r][...]], axis=0)
            both = nn(own, w_ref[:, : 2 * ff])
            gate, up = both[:, :ff], both[:, ff:]
            sig = jax.nn.sigmoid(gate)
            mixed = (gate * sig * up).astype(jnp.bfloat16)
            mixed_ref[low, :] = mixed[:rows]
            mixed_ref[high, :] = mixed[rows:]
            grad_mixed = nn(cot, w_ref[:, 2 * ff :])
            grad_gate = (grad_mixed * up * sig * (1.0 + gate * (1.0 - sig))).astype(jnp.bfloat16)
            grad_up = (grad_mixed * gate * sig).astype(jnp.bfloat16)
            grad = jnp.concatenate([grad_gate, grad_up], axis=1)
            grad_ref[low, :] = grad[:rows]
            grad_ref[high, :] = grad[rows:]
            product = nt(grad, w_ref[:, : 2 * ff])
            mine_ref[low, :] = product[:rows]
            other_ref[low, :] = product[rows:].astype(jnp.bfloat16)

    outs = [
        ((tokens, width), jnp.bfloat16),
        ((tokens, ff), jnp.bfloat16),
        ((tokens, 2 * ff), jnp.bfloat16),
        ((half, width), jnp.float32),
        ((half, width), jnp.bfloat16),
    ]
    return call(body, outs, (*blocks, *cot_blocks, weight))


def attention_backward(
    blocks, weight, raw, rotated, value, probs, attended, gain_q, gain_k, cosine, sinusoid, sizes
):
    team, rows, heads_q, heads_kv = sizes
    width = weight.shape[0]
    q_cols, kv_cols = heads_q * HEAD_SIZE, heads_kv * HEAD_SIZE
    per_kv = heads_q // heads_kv
    half, group = team * rows, 2 * rows
    tokens = team * group
    scale = HEAD_SIZE ** (-0.5)

    def body(*refs):
        m = refs[: 2 * team]
        (
            w_ref, raw_ref, qk_ref, v_ref, p_ref, att_ref, gq_ref, gk_ref, cos_ref, sin_ref,
        ) = refs[2 * team : 2 * team + 10]
        all_ref, grad_ref, gain_ref = refs[2 * team + 10 :]
        gain_sums = [jnp.zeros((1, HEAD_SIZE), jnp.float32) for _ in range(2)]
        for r in range(team):
            low = slice(r * rows, (r + 1) * rows)
            high = slice(half + r * rows, half + (r + 1) * rows)
            span = slice(r * group, (r + 1) * group)
            own = jnp.concatenate([m[r][...], m[team + r][...]], axis=0)
            all_ref[low, :] = own[:rows]
            all_ref[high, :] = own[rows:]
            grad_att = nn(own, w_ref[:, q_cols + 2 * kv_cols :]).astype(jnp.bfloat16)
            att = jnp.concatenate([att_ref[low, :], att_ref[high, :]], axis=0)
            cos, sin = cos_ref[span, :], sin_ref[span, :]
            grads = [None] * (heads_q + 2 * heads_kv)

            def into(at, piece):
                grads[at] = piece if grads[at] is None else grads[at] + piece

            for h in range(heads_q):
                kv = h // per_kv
                out_grad = grad_att[:, head(h)]
                at = (r * heads_q + h) * group
                p = p_ref[at : at + group, :]
                grad_p = nt(out_grad, v_ref[span, head(kv)])
                delta = jnp.sum(
                    out_grad.astype(jnp.float32) * att[:, head(h)].astype(jnp.float32),
                    axis=-1,
                    keepdims=True,
                )
                grad_s = (p * (grad_p - delta) * scale).astype(jnp.bfloat16)
                into(h, nn(grad_s, qk_ref[span, head(heads_q + kv)]))
                into(heads_q + kv, tn(grad_s, qk_ref[span, head(h)]))
                into(heads_q + heads_kv + kv, tn(p.astype(jnp.bfloat16), out_grad))
            for h in range(heads_q + 2 * heads_kv):
                piece = grads[h]
                if h < heads_q + heads_kv:
                    kind = 0 if h < heads_q else 1
                    gain = gq_ref[...] if kind == 0 else gk_ref[...]
                    before = raw_ref[span, head(h)]
                    inv = inverse_rms(before)
                    turned = piece * cos + pltpu.roll(piece * sin, HEAD_SIZE // 2, 1)
                    unit = before * inv
                    gain_sums[kind] = gain_sums[kind] + jnp.sum(
                        turned * unit, axis=0, keepdims=True
                    )
                    scaled = turned * gain
                    piece = inv * (
                        scaled - unit * jnp.mean(scaled * unit, axis=-1, keepdims=True)
                    )
                piece = piece.astype(jnp.bfloat16)
                grad_ref[low, head(h)] = piece[:rows]
                grad_ref[high, head(h)] = piece[rows:]
        gain_ref[0:1, :] = gain_sums[0]
        gain_ref[1:2, :] = gain_sums[1]

    outs = [
        ((tokens, width), jnp.bfloat16),
        ((tokens, q_cols + 2 * kv_cols), jnp.bfloat16),
        ((2, HEAD_SIZE), jnp.float32),
    ]
    args = (
        *blocks, weight, raw, rotated, value, probs, attended, gain_q, gain_k, cosine, sinusoid,
    )
    return call(body, outs, args)


def dot_rows(a, b):
    return lax.dot_general(a, b, (((0,), (0,)), ((), ())), preferred_element_type=jnp.float32)


def dot_cols(a, b):
    return lax.dot_general(a, b, (((1,), (1,)), ((), ())), preferred_element_type=jnp.float32)


def after(value, *others):
    return lax.optimization_barrier((value, *others))[0]


class Layout:
    def __init__(self, dp, tensor, team):
        self.dp, self.tensor, self.team, self.line = dp, tensor, team, dp // team
        index = lax.axis_index("dp")
        self.index = index
        self.z = index // team
        self.t = index % team
        self.core = lax.axis_index("tensor")

    def to_peer(self, value, r):
        team = self.team
        pairs = [(i, (i // team) * team + ((i % team) ^ r)) for i in range(self.dp)]
        return lax.ppermute(value, "dp", pairs)

    def to_core(self, value):
        return lax.ppermute(value, "tensor", [(0, 1), (1, 0)])

    def xor_order(self, blocks):
        blocks = list(blocks)
        bit = 1
        while bit < self.team:
            odd = (self.t & bit) != 0
            blocks = [jnp.where(odd, blocks[r ^ bit], blocks[r]) for r in range(self.team)]
            bit *= 2
        return blocks

    def gather_tokens(self, own):
        mine = [own] + [self.to_peer(own, r) for r in range(1, self.team)]
        return mine, [self.to_core(part) for part in mine]

    def scatter_tokens(self, mine, other):
        rows = self.rows
        summed = mine + self.to_core(other).astype(jnp.float32)
        total = summed[:rows]
        for r in range(1, self.team):
            piece = summed[r * rows : (r + 1) * rows].astype(jnp.bfloat16)
            total = total + self.to_peer(piece, r).astype(jnp.float32)
        return total

    def trade_columns(self, blocks):
        relative = self.xor_order(blocks)
        got = [relative[0]] + [self.to_peer(relative[r], r) for r in range(1, self.team)]
        return jnp.concatenate(self.xor_order(got), axis=0)

    def lines(self):
        return [[z * self.team + t for z in range(self.line)] for t in range(self.team)]

    def line_gather(self, block):
        return lax.all_gather(block, "dp", axis=0, tiled=True, axis_index_groups=self.lines())

    def line_scatter(self, grad):
        return lax.psum_scatter(
            grad.astype(jnp.bfloat16),
            "dp",
            scatter_dimension=0,
            tiled=True,
            axis_index_groups=self.lines(),
        ).astype(jnp.float32)

    def return_columns(self, summed):
        rows = summed.shape[0] // self.team
        blocks = [summed[s * rows : (s + 1) * rows] for s in range(self.team)]
        relative = self.xor_order(blocks)
        got = [relative[0]]
        for r in range(1, self.team):
            got.append(
                self.to_peer(relative[r].astype(jnp.bfloat16), r).astype(jnp.float32)
            )
        return self.xor_order(got)

    def gather_small(self, value):
        if self.dp & (self.dp - 1):
            return lax.all_gather(value[None, :], "dp", axis=0, tiled=True)
        full = value[None, :]
        bit = 1
        while bit < self.dp:
            other = lax.ppermute(full, "dp", [(i, i ^ bit) for i in range(self.dp)])
            odd = (self.index & bit) != 0
            full = jnp.where(
                odd,
                jnp.concatenate([other, full], axis=0),
                jnp.concatenate([full, other], axis=0),
            )
            bit *= 2
        return full

    def sum_small(self, value):
        if self.dp & (self.dp - 1):
            return lax.psum(value, ("dp", "tensor"))
        value = value + self.to_core(value)
        bit = 1
        while bit < self.dp:
            value = value + lax.ppermute(value, "dp", [(i, i ^ bit) for i in range(self.dp)])
            bit *= 2
        return value


def split_columns(weight, team):
    width = weight.shape[1] // team
    return [weight[:, s * width : (s + 1) * width] for s in range(team)]


def make_body(dp, tensor):
    def per_device(
        hidden_in,
        positions,
        w_query,
        w_key,
        w_value,
        w_output,
        w_gate,
        w_up,
        w_down,
        norm_gains,
        grad_out,
    ):
        rows, width = hidden_in.shape
        group = positions.shape[0]
        team = math.gcd(dp, w_key.shape[1] // HEAD_SIZE)
        lay = Layout(dp, tensor, team)
        lay.rows = rows
        heads_kv = w_key.shape[1] // HEAD_SIZE // team
        heads_q = w_query.shape[1] // HEAD_SIZE // team
        q_cols, kv_cols = heads_q * HEAD_SIZE, heads_kv * HEAD_SIZE
        ff = w_gate.shape[1] // team
        tokens = team * group

        def merge(*weights):
            pieces = [split_columns(w, team) for w in weights]
            return [jnp.concatenate([p[s] for p in pieces], axis=1) for s in range(team)]

        attn_block = lay.trade_columns(merge(w_query, w_key, w_value, w_output.T))
        attn_w = lay.line_gather(attn_block)
        in_mine, in_other = lay.gather_tokens(after(hidden_in, attn_block))
        small = lay.gather_small(
            after(jnp.concatenate([norm_gains, positions.astype(jnp.float32)]), attn_block)
        )
        gains = small[:, : norm_gains.shape[0]].reshape(-1)
        team_seats = lax.dynamic_slice_in_dim(
            small[:, norm_gains.shape[0] :], lay.z * team, team, axis=0
        )
        gate_late, up_late, down_late, *_ = lax.optimization_barrier(
            (w_gate, w_up, w_down, *in_mine)
        )
        ffn_block = lay.trade_columns(merge(gate_late, up_late, down_late.T))
        ffn_w = lay.line_gather(ffn_block)
        cot_mine, cot_other = lay.gather_tokens(after(grad_out, ffn_block))

        gain_attn = gains[:width]
        gain_ffn = gains[width : 2 * width]
        gain_q = gains[2 * width : 2 * width + HEAD_SIZE][None, :]
        gain_k = gains[2 * width + HEAD_SIZE :][None, :]

        def own_first(v):
            low, high = v[..., :rows], v[..., rows:]
            first = lay.core == 0
            return jnp.concatenate(
                [jnp.where(first, low, high), jnp.where(first, high, low)], axis=-1
            )

        seats = own_first(
            jnp.concatenate(
                lay.xor_order([team_seats[s : s + 1] for s in range(team)]), axis=0
            )
        )
        place = own_first(jnp.arange(group, dtype=jnp.int32))
        query_place = place[None, :, None]
        key_place = place[None, None, :]
        first_seen = query_place - seats.astype(jnp.int32)[:, :, None]
        seen = (key_place <= query_place) & (key_place >= first_seen)
        hide = jnp.where(seen, 0.0, -1.0).astype(jnp.float32).reshape(tokens, group)
        cosine, sinusoid = rope_tables(seats.reshape(-1))

        sizes = (team, rows, heads_q, heads_kv)
        normed, raw, rotated, value, probs, attended, att_mine, att_other = attention_forward(
            in_mine + in_other, attn_w, gain_attn[None, :], gain_q, gain_k, cosine, sinusoid,
            hide, sizes,
        )
        mid = hidden_in.astype(jnp.float32) + lay.scatter_tokens(att_mine, att_other)
        normed_own, ffn_back = jax.vjp(rms_scale, mid, gain_ffn)
        ffn_mine, ffn_other = lay.gather_tokens(normed_own.astype(jnp.bfloat16))
        ffn_in, mixed, grad_both, gnf_mine, gnf_other = ffn_both(
            ffn_mine + ffn_other, cot_mine + cot_other, ffn_w, team, rows
        )
        cot = jnp.concatenate(cot_mine + cot_other, axis=0)
        half = team * rows
        ffn_part = jnp.concatenate(
            [dot_rows(ffn_in, grad_both), dot_rows(cot, mixed)], axis=1
        ).astype(jnp.bfloat16)
        grad_ffn = lay.line_scatter(ffn_part)
        grad_normed_ffn = lay.scatter_tokens(gnf_mine, gnf_other)
        grad_mid_norm, grad_gain_ffn = ffn_back(grad_normed_ffn)
        grad_mid = grad_out.astype(jnp.float32) + grad_mid_norm
        mid_mine, mid_other = lay.gather_tokens(grad_mid.astype(jnp.bfloat16))
        mixed_late, *_ = lax.optimization_barrier((mixed, *mid_mine))
        down_w = ffn_w[:, 2 * ff :]
        hidden_out = (
            mid
            + lay.scatter_tokens(
                dot_cols(mixed_late[:half], down_w),
                dot_cols(mixed_late[half:], down_w).astype(jnp.bfloat16),
            )
        ).astype(jnp.bfloat16)

        grad_mid_all, grad_qkv, gain_qk = attention_backward(
            mid_mine + mid_other, attn_w, raw, rotated, value, probs, attended, gain_q, gain_k,
            cosine, sinusoid, sizes,
        )
        attn_part = jnp.concatenate(
            [dot_rows(normed, grad_qkv), dot_rows(grad_mid_all, attended)], axis=1
        ).astype(jnp.bfloat16)
        grad_qkv_w = lay.return_columns(lay.line_scatter(attn_part))
        grad_qkv, grad_ffn, _ = lax.optimization_barrier((grad_qkv, grad_ffn, attn_part))
        qkv_w = attn_w[:, : q_cols + 2 * kv_cols]
        grad_normed_attn = lay.scatter_tokens(
            dot_cols(grad_qkv[:half], qkv_w),
            dot_cols(grad_qkv[half:], qkv_w).astype(jnp.bfloat16),
        )
        _, attn_back = jax.vjp(rms_scale, hidden_in.astype(jnp.float32), gain_attn)
        grad_in_norm, grad_gain_attn = attn_back(grad_normed_attn)
        grad_in = (grad_mid + grad_in_norm).astype(jnp.bfloat16)
        grad_ffn = lay.return_columns(grad_ffn)

        gain_parts = jnp.concatenate(
            [
                grad_gain_attn,
                grad_gain_ffn,
                gain_qk.reshape(-1),
            ]
        )
        gain_total = lay.sum_small(gain_parts)
        share = gain_total.shape[0] // (dp * tensor)
        seat = lay.index * tensor + lay.core
        grad_gains = lax.dynamic_slice_in_dim(gain_total, seat * share, share, axis=0)

        def columns(blocks, lo, hi):
            return jnp.concatenate([b[:, lo:hi] for b in blocks], axis=1)

        return (
            hidden_out,
            grad_in,
            columns(grad_qkv_w, 0, q_cols),
            columns(grad_qkv_w, q_cols, q_cols + kv_cols),
            columns(grad_qkv_w, q_cols + kv_cols, q_cols + 2 * kv_cols),
            columns(grad_qkv_w, q_cols + 2 * kv_cols, 2 * q_cols + 2 * kv_cols).T,
            columns(grad_ffn, 0, ff),
            columns(grad_ffn, ff, 2 * ff),
            columns(grad_ffn, 2 * ff, 3 * ff).T,
            grad_gains,
        )

    return per_device


def solution(mesh):
    placed = (
        P(("dp", "tensor"), None),
        P("dp"),
        P("dp", "tensor"),
        P("dp", "tensor"),
        P("dp", "tensor"),
        P("tensor", "dp"),
        P("dp", "tensor"),
        P("dp", "tensor"),
        P("tensor", "dp"),
        P("dp"),
        P(("dp", "tensor"), None),
    )
    return jax.shard_map(
        make_body(mesh.shape["dp"], mesh.shape["tensor"]),
        mesh=mesh,
        in_specs=placed,
        out_specs=(
            P(("dp", "tensor"), None),
            P(("dp", "tensor"), None),
            P("dp", "tensor"),
            P("dp", "tensor"),
            P("dp", "tensor"),
            P("tensor", "dp"),
            P("dp", "tensor"),
            P("dp", "tensor"),
            P("tensor", "dp"),
            P(("dp", "tensor")),
        ),
        check_vma=False,
    )
```
